32 devices in a mesh: len: 8 (over z, y), wire: 4 (over x, core).
Axes of the slice: x: 2, y: 2, z: 4, core: 2. Of those that a mesh axis runs over, the one named last changes fastest.
Arguments:
- displacement: float32 [8, 4, 3, 3584], P('len', 'wire'), may hold values from -6 to 6
- previous: float32 [8, 4, 3, 3584], P('len', 'wire'), may hold values from -6 to 6
- element_nodes: int32 [8, 4, 125, 64], P('len', 'wire'), may hold values from 0 to 223
- element_stiffness: float32 [8, 4, 64], P('len', 'wire'), may hold values from 0.5 to 2
- gradient_op: float32 [375, 125], replicated, may hold values from -0.5 to 0.5
- mass_partial: float32 [8, 4, 3584], P('len', 'wire'), may hold values from 0.5 to 2
- left_ghost: int32 [8, 4, 768], P('len', 'wire'), may hold values from 0 to 3583, as said below
- right_ghost: int32 [8, 4, 768], P('len', 'wire'), may hold values from 0 to 3583, as said below
- contact_slots: int32 [8, 4, 4, 2048], P('len', 'wire'), may hold values from 0 to 3583
- contact_live: int32 [8, 4, 4, 2048], P('len', 'wire'), may hold values from 0 to 1, as said below
Outputs:
- final_field: float32 [8, 4, 3, 3584], P('len', 'wire')
- prior_field: float32 [8, 4, 3, 3584], P('len', 'wire')
The draws below stay inside these ranges and needn't reach their ends.
Inputs may be any that keep to these rules, and one draw needn't show every extreme that they name: Within one piece the 768 slots of left_ghost and the 768 slots of right_ghost are all distinct. Within one piece the 768 slots of right_ghost and those of left_ghost are all distinct. contact_live[l, w, q, k] equals contact_live[l, q, w, k], and is 0 where q = w.
All inputs are finite; a program needn't handle non-finite values.
Results may differ from the reference program's by a relative error of at most 0.0003.
Values sent between devices are 32-bit elements; how exact they have to be, the bound alone decides.
A program may use at most 64 MiB of HBM per device.

```python
import math
import jax
import jax.numpy as jnp
from jax import lax

NPE = 125
E_DEV = 64
GHOST = 768
CPAIR = 2048
ITERS = 4
NODES = 3584
NGRAD = 375
SEGS = 8
WIRES = 4


def shuffled_slots(key):
    device_keys = jax.random.split(jax.random.fold_in(key, 11), SEGS * WIRES)
    shuffled = jax.vmap(lambda one_key: jax.random.permutation(one_key, NODES))(device_keys)
    return shuffled.reshape(SEGS, WIRES, NODES)


def draw_left_ghost(key, part):
    return shuffled_slots(key)[:, :, :GHOST].astype(jnp.int32)


def draw_right_ghost(key, part):
    return shuffled_slots(key)[:, :, GHOST:2 * GHOST].astype(jnp.int32)


def draw_contact_live(key, part):
    rate_key, bits_key = jax.random.split(jax.random.fold_in(key, 23))
    live_rate = jax.random.randint(rate_key, (SEGS, WIRES, WIRES, 1), 20, 101)
    random_bits = jax.random.randint(bits_key, (SEGS, WIRES, WIRES, CPAIR), 0, 100)
    upper_half = (random_bits < live_rate).astype(jnp.int32)
    mirrored = jnp.transpose(upper_half, (0, 2, 1, 3))
    wire_ids = jnp.arange(WIRES)
    above_diag = (wire_ids[:, None] < wire_ids[None, :])[None, :, :, None]
    below_diag = (wire_ids[:, None] > wire_ids[None, :])[None, :, :, None]
    return jnp.where(above_diag, upper_half, jnp.where(below_diag, mirrored, 0)).astype(jnp.int32)


def with_ends(drawn, rng, least, high):
    shape = drawn.shape
    place = [jax.random.randint(jax.random.fold_in(rng, axis), (), 0, shape[axis]) for axis in range(len(shape))]
    drawn = drawn.at[tuple(place)].set(least)
    longest = shape.index(max(shape))
    place[longest] = (place[longest] + 1) % shape[longest]
    return drawn.at[tuple(place)].set(high)


def shard_levels(key, extent, pieces, low, largest):
    factor_of, own = 1.0, jax.random.fold_in(key, 6)
    for position, parts in pieces:
        heights = jnp.exp(jax.random.uniform(jax.random.fold_in(own, position), (parts,), jnp.float32, low / len(pieces), largest / len(pieces)))
        factor_of = factor_of * jnp.repeat(heights, extent[position] // parts).reshape([-1 if axis == position else 1 for axis in range(len(extent))])
    return factor_of


def scatter_about(key, extent, scale, limit, cuts=(), kind=jnp.bfloat16):
    entries = scale * jax.random.normal(key, extent, jnp.float32)
    if cuts:
        entries = entries * shard_levels(key, extent, cuts, -0.22, 0.18)
    return jnp.clip(entries, -limit, limit).astype(kind)


def setup_inputs(seed: int = 0) -> dict:
    seeds = jax.random.split(jax.random.key(seed), 11)
    return {
        "displacement": scatter_about(seeds[0], (SEGS, WIRES, 3, NODES), 1.0, 6.0, ((0, 8), (1, 4)), jnp.float32),
        "previous": scatter_about(seeds[1], (SEGS, WIRES, 3, NODES), 1.0, 6.0, ((0, 8), (1, 4)), jnp.float32),
        "element_nodes": with_ends(jax.random.randint(seeds[2], (SEGS, WIRES, NPE, E_DEV), 0, 224), jax.random.fold_in(seeds[2], 1), 0, 223).astype(jnp.int32),
        "element_stiffness": jnp.clip(jnp.exp(math.log(2.0) - 1.3862944 * jax.random.uniform(seeds[3], (SEGS, WIRES, E_DEV), jnp.float32) ** shard_levels(seeds[3], (SEGS, WIRES, E_DEV), ((0, 8), (1, 4)), -0.2, 0.2)), 0.5, 2.0),
        "gradient_op": scatter_about(seeds[4], (NGRAD, NPE), NPE ** -0.5, 0.5, (), jnp.float32),
        "mass_partial": jnp.clip(jnp.exp(math.log(2.0) - 1.3862944 * jax.random.uniform(seeds[5], (SEGS, WIRES, NODES), jnp.float32) ** shard_levels(seeds[5], (SEGS, WIRES, NODES), ((0, 8), (1, 4)), -0.2, 0.2)), 0.5, 2.0),
        "left_ghost": draw_left_ghost(jax.random.fold_in(seeds[10], 71), 0),
        "right_ghost": draw_right_ghost(jax.random.fold_in(seeds[10], 71), 0),
        "contact_slots": with_ends(jax.random.randint(seeds[8], (SEGS, WIRES, WIRES, CPAIR), 0, NODES), jax.random.fold_in(seeds[8], 1), 0, NODES - 1).astype(jnp.int32),
        "contact_live": draw_contact_live(jax.random.fold_in(seeds[10], 71), 0),
    }


PENALTY = 4.0
TIME_SQUARE = 0.03
block_elements = 4
block_slots = 224


def take_slots(field, slots):
    return field[:, slots]


def add_slots(field, slots, values):
    return field.at[:, slots].add(values)


def element_force(field, local_nodes, stiffness, gradient_op):
    offsets = (jnp.arange(local_nodes.shape[1], dtype=jnp.int32) // block_elements) * block_slots
    nodes = (local_nodes + offsets[None, :]).astype(jnp.int32)
    element_field = field[:, nodes]
    gradients = jnp.einsum("gn,cne->cge", gradient_op, element_field, precision=lax.Precision.HIGHEST)
    stresses = gradients * stiffness[None, None, :]
    element_out = jnp.einsum("gn,cge->cne", gradient_op, stresses, precision=lax.Precision.HIGHEST)
    return jnp.zeros_like(field).at[:, nodes].add(-element_out)


def assemble(partial_value, left_ghost, right_ghost):
    take_all = jax.vmap(jax.vmap(take_slots))
    add_all = jax.vmap(jax.vmap(add_slots))
    left_send = take_all(partial_value, left_ghost)
    right_send = take_all(partial_value, right_ghost)
    blank = jnp.zeros_like(left_send[:1])
    from_prev = jnp.concatenate([blank, right_send[:-1]], axis=0)
    from_next = jnp.concatenate([left_send[1:], blank], axis=0)
    partial_value = add_all(partial_value, left_ghost, from_prev)
    return add_all(partial_value, right_ghost, from_next)


def reference(displacement, previous, element_nodes, element_stiffness, gradient_op, mass_partial, left_ghost, right_ghost, contact_slots, contact_live):
    mass = assemble(mass_partial[:, :, None, :], left_ghost, right_ghost)
    flat_slots = contact_slots.reshape(SEGS, WIRES, WIRES * CPAIR)
    live = contact_live.astype(jnp.float32)[:, :, None, :, :]
    per_wire = jax.vmap(element_force, in_axes=(0, 0, 0, None))

    def segment_force(group):
        return per_wire(group[0], group[1], group[2], gradient_op)

    for turn_index in range(ITERS):
        force = lax.map(segment_force, (displacement, element_nodes, element_stiffness))
        sent = jax.vmap(jax.vmap(take_slots))(displacement, flat_slots).reshape(SEGS, WIRES, 3, WIRES, CPAIR)
        received = jnp.transpose(sent, (0, 3, 2, 1, 4))
        penalty = (PENALTY * live * (received - sent)).reshape(SEGS, WIRES, 3, WIRES * CPAIR)
        force = jax.vmap(jax.vmap(add_slots))(force, flat_slots, penalty)
        force = assemble(force, left_ghost, right_ghost)
        stepped = 2.0 * displacement - previous + TIME_SQUARE * force / mass
        previous, displacement = displacement, stepped
    return displacement, previous
```

```python
import functools

import jax
import jax.numpy as jnp
from jax import lax
from jax.experimental import pallas as pl
from jax.experimental.pallas import tpu as pltpu
from jax.sharding import PartitionSpec as P

ITERS = 4
PENALTY = 4.0
TIME_SQUARE = 0.03
block_slots = 224
block_elements = 4
LANES = 128
SUB = 8
f32 = jnp.float32
bf16 = jnp.bfloat16
MESH = pl.DeviceIdType.MESH


def round_up(value, step):
    return -(-value // step) * step


def dot(a, b):
    return jnp.dot(a, b, preferred_element_type=f32)


def dot_nt(a, b):
    return lax.dot_general(a, b, (((1,), (1,)), ((), ())), preferred_element_type=f32)


def block_kernel(grad_ref, nodes_ref, stiff_ref, out_ref, gram):
    node_count = grad_ref.shape[1]
    node_pad = gram.shape[0]
    wide = out_ref.shape[1]

    @pl.when(pl.program_id(0) == 0)
    def _():
        op = grad_ref[...]
        product = lax.dot_general(
            op, op, (((0,), (0,)), ((), ())), precision=lax.Precision.HIGHEST, preferred_element_type=f32
        )
        high = product.astype(bf16)
        gram[...] = jnp.zeros_like(gram)
        gram[:node_count, :node_count] = high
        gram[:node_count, node_pad : node_pad + node_count] = (product - high.astype(f32)).astype(bf16)

    nodes = nodes_ref[0]
    slot_ids = lax.broadcasted_iota(jnp.int32, (wide, nodes.shape[1]), 0)
    onehot = jnp.where(slot_ids == nodes, 1.0, 0.0).astype(bf16)
    pieces = []
    for e in range(block_elements):
        both = dot(onehot[:, e * node_pad : (e + 1) * node_pad], gram[...])
        pieces.append(both[:, :node_pad] + both[:, node_pad:])
    columns = jnp.concatenate(pieces, axis=1) * stiff_ref[0]
    high = columns.astype(bf16)
    low = (columns - high.astype(f32)).astype(bf16)
    operator = dot_nt(high, onehot) + dot_nt(low, onehot)
    high = operator.astype(bf16)
    out_ref[0, :, :wide] = high
    out_ref[0, :, wide:] = (operator - high.astype(f32)).astype(bf16)


def step_kernel(
    others,
    segments,
    chunk,
    u_in, p_in, mass_ref, op_ref, cb_ref, ci_ref, gb_ref, gi_ref,
    u_ref, p_ref,
    c_hot, g_hot, part, c_send, c_recv, g_send, g_recv,
    c_ssem, c_rsem, g_ssem, g_rsem,
):
    blocks = op_ref.shape[0]
    rows, wide = u_in.shape
    wires = others + 1
    pairs = cb_ref.shape[1] // others
    ghosts = gb_ref.shape[1] // 2
    me = lax.axis_index("wire")
    seg = lax.axis_index("len")
    has_prev = seg > 0
    has_next = seg < segments - 1

    def partner(d):
        return lax.rem(me + (d + 1), wires)

    barrier = pltpu.get_barrier_semaphore()
    for d in range(others):
        pl.semaphore_signal(barrier, inc=1, device_id={"wire": partner(d)}, device_id_type=MESH)

    @pl.when(has_prev)
    def _():
        pl.semaphore_signal(barrier, inc=1, device_id={"len": seg - 1}, device_id_type=MESH)

    @pl.when(has_next)
    def _():
        pl.semaphore_signal(barrier, inc=1, device_id={"len": seg + 1}, device_id_type=MESH)

    def fill(hot, index_ref):
        count = index_ref.shape[1]
        step = 512 if count % 512 == 0 else LANES

        def body(i, _):
            cols = pl.ds(pl.multiple_of(i * step, step), step)
            ids = lax.broadcasted_iota(jnp.int32, (wide, step), 0)
            hot[:, cols] = jnp.where(ids == index_ref[:, cols], 1.0, 0.0).astype(bf16)
            return 0

        lax.fori_loop(0, count // step, body, 0)

    fill(c_hot, ci_ref)
    fill(g_hot, gi_ref)
    u_ref[...] = u_in[...]
    p_ref[...] = p_in[...]

    @pl.when(jnp.logical_not(has_prev))
    def _():
        g_recv[:, 0] = jnp.zeros((ITERS,) + g_recv.shape[2:], f32)

    @pl.when(jnp.logical_not(has_next))
    def _():
        g_recv[:, 1] = jnp.zeros((ITERS,) + g_recv.shape[2:], f32)

    last = segments - 1
    pl.semaphore_wait(
        barrier, others + lax.div(seg + last, segments) + lax.div(last - seg + last, segments)
    )

    row_all = lax.broadcasted_iota(jnp.int32, (rows, wide), 0) & (SUB - 1)
    low_all = row_all < 4

    def rows_of(width):
        return lax.broadcasted_iota(jnp.int32, (SUB, width), 0)

    def split(x):
        high = x.astype(bf16).astype(f32)
        return jnp.where(low_all, high, pltpu.roll(x - high, 4, 0)).astype(bf16)

    def take(packed, hot, base_ref, start, width):
        cols = slice(start, start + width)
        picked = dot(packed, hot[:, cols])
        which = jnp.broadcast_to(base_ref[:, cols], (SUB, width))
        total = jnp.zeros((SUB, width), f32)
        for b in range(blocks):
            total = jnp.where(which == b, picked[b * SUB : (b + 1) * SUB], total)
        return total + pltpu.roll(total, 4, 0)

    def put(values, hot, base_ref, start, width):
        cols = slice(start, start + width)
        high = values.astype(bf16).astype(f32)
        values = jnp.where(rows_of(width) < 4, high, values - high)
        which = jnp.broadcast_to(base_ref[:, cols], (SUB, width))
        spread = jnp.concatenate([jnp.where(which == b, values, 0.0) for b in range(blocks)], axis=0)
        return dot_nt(spread.astype(bf16), hot[:, cols])

    def take_list(packed, hot, base_ref, start, count, out_ref):
        half = count // 2
        width = chunk if half % chunk == 0 else half
        for at in range(0, half, width):
            first = take(packed, hot, base_ref, start + at, width)
            second = take(packed, hot, base_ref, start + half + at, width)
            out_ref[:, at : at + width] = jnp.where(rows_of(width) < 4, first, second)

    def put_list(values, hot, base_ref, start, count, total):
        half = count // 2
        width = chunk if half % chunk == 0 else half
        for at in range(0, half, width):
            here = values[:, at : at + width]
            turned = pltpu.roll(here, 4, 0)
            low = rows_of(width) < 4
            total = total + put(jnp.where(low, here, turned), hot, base_ref, start + at, width)
            total = total + put(jnp.where(low, turned, here), hot, base_ref, start + half + at, width)
        return total

    def contact_copy(step, d):
        return pltpu.make_async_remote_copy(
            src_ref=c_send.at[d],
            dst_ref=c_recv.at[step, others - 1 - d],
            send_sem=c_ssem.at[d],
            recv_sem=c_rsem.at[step, others - 1 - d],
            device_id={"wire": partner(d)},
            device_id_type=MESH,
        )

    def contact_arrival(step, d):
        return pltpu.make_async_remote_copy(
            src_ref=c_send.at[d],
            dst_ref=c_recv.at[step, d],
            send_sem=c_ssem.at[d],
            recv_sem=c_rsem.at[step, d],
            device_id={"wire": partner(d)},
            device_id_type=MESH,
        )

    def ghost_copy(step, side):
        return pltpu.make_async_remote_copy(
            src_ref=g_send.at[side],
            dst_ref=g_recv.at[step, 1 - side],
            send_sem=g_ssem.at[side],
            recv_sem=g_rsem.at[step, 1 - side],
            device_id={"len": seg - 1 if side == 0 else seg + 1},
            device_id_type=MESH,
        )

    def ghost_arrival(step, side):
        return pltpu.make_async_remote_copy(
            src_ref=g_send.at[side],
            dst_ref=g_recv.at[step, side],
            send_sem=g_ssem.at[side],
            recv_sem=g_rsem.at[step, side],
            device_id={"len": seg - 1 if side == 0 else seg + 1},
            device_id_type=MESH,
        )

    exists = (has_prev, has_next)

    def one_step(step, _):
        packed = split(u_ref[...])
        for d in range(others):
            take_list(packed, c_hot, cb_ref, d * pairs, pairs, c_send.at[d])
            contact_copy(step, d).start()

        for b in range(blocks):
            pair = packed[(b // 2) * 2 * SUB : (b // 2 + 1) * 2 * SUB]
            out = dot(pair, op_ref[b])[(b % 2) * SUB : (b % 2 + 1) * SUB]
            main = out[:, :wide]
            part[b * SUB : (b + 1) * SUB, :] = main + pltpu.roll(main, 4, 0) + out[:, wide:]

        spread = jnp.zeros((rows, wide), f32)
        for d in range(others):
            contact_arrival(step, d).wait_recv()
            spread = put_list(c_recv[step, d] - c_send[d], c_hot, cb_ref, d * pairs, pairs, spread)
        spread = spread + pltpu.roll(spread, rows - 4, 0)
        local = jnp.where(row_all < 3, PENALTY * spread - part[...], mass_ref[...])
        part[...] = local

        packed = split(local)
        for side in range(2):
            take_list(packed, g_hot, gb_ref, side * ghosts, ghosts, g_send.at[side])

            @pl.when(exists[side])
            def _():
                ghost_copy(step, side).start()

        spread = jnp.zeros((rows, wide), f32)
        for side in range(2):

            @pl.when(exists[side])
            def _():
                ghost_arrival(step, side).wait_recv()

            spread = put_list(g_recv[step, side], g_hot, gb_ref, side * ghosts, ghosts, spread)
        spread = spread + pltpu.roll(spread, rows - 4, 0)
        total = jnp.where(low_all, part[...] + spread, 0.0)
        for b in range(blocks):
            at = slice(b * SUB, (b + 1) * SUB)
            force = total[at]
            mass = jnp.broadcast_to(force[3:4], force.shape)
            now = u_ref[at, :]
            stepped = 2.0 * now - p_ref[at, :] + TIME_SQUARE * force / mass
            p_ref[at, :] = now
            u_ref[at, :] = jnp.where(rows_of(wide) < 3, stepped, 0.0)

        for d in range(others):
            contact_copy(step, d).wait_send()
        for side in range(2):

            @pl.when(exists[side])
            def _():
                ghost_copy(step, side).wait_send()

        return 0

    lax.fori_loop(0, ITERS, one_step, 0)


def on_device(
    displacement, previous, element_nodes, element_stiffness, gradient_op,
    mass_partial, left_ghost, right_ghost, contact_slots, contact_live,
):
    nodes = element_nodes[0, 0]
    node_count, elements = nodes.shape
    blocks = elements // block_elements
    wide = round_up(block_slots, 2 * LANES)
    node_pad = round_up(node_count, LANES)
    segments = lax.axis_size("len")
    wires = lax.axis_size("wire")
    others = wires - 1
    me = lax.axis_index("wire")
    slots = displacement.shape[3]
    parts = displacement.shape[2]
    rows = blocks * SUB

    nodes_t = jnp.pad(nodes.T, ((0, 0), (0, node_pad - node_count)), constant_values=-1)
    nodes_t = nodes_t.reshape(blocks, 1, block_elements * node_pad)
    stiff = jnp.repeat(element_stiffness[0, 0], node_pad).reshape(blocks, 1, block_elements * node_pad)

    vmem = pl.BlockSpec(memory_space=pltpu.VMEM)
    operators = pl.pallas_call(
        block_kernel,
        grid=(blocks,),
        out_shape=jax.ShapeDtypeStruct((blocks, wide, 2 * wide), bf16),
        in_specs=[
            pl.BlockSpec(gradient_op.shape, lambda b: (0, 0)),
            pl.BlockSpec((1, 1, block_elements * node_pad), lambda b: (b, 0, 0)),
            pl.BlockSpec((1, 1, block_elements * node_pad), lambda b: (b, 0, 0)),
        ],
        out_specs=pl.BlockSpec((1, wide, 2 * wide), lambda b: (b, 0, 0)),
        scratch_shapes=[pltpu.VMEM((node_pad, 2 * node_pad), bf16)],
        name="operators",
    )(gradient_op, nodes_t, stiff)

    def lay(field, row):
        count = field.shape[0]
        field = field.reshape(count, blocks, block_slots).transpose(1, 0, 2)
        return jnp.pad(field, ((0, 0), (row, SUB - row - count), (0, wide - block_slots)))

    u = lay(displacement[0, 0], 0).reshape(rows, wide)
    p = lay(previous[0, 0], 0).reshape(rows, wide)
    mass = mass_partial[0, 0].reshape(blocks, 1, block_slots)
    mass = jnp.pad(mass, ((0, 0), (0, 0), (0, wide - block_slots)), constant_values=1.0)
    mass = jnp.pad(mass, ((0, 0), (3, SUB - 4), (0, 0))).reshape(rows, wide)

    def from_me(x):
        return lax.dynamic_slice_in_dim(jnp.concatenate([x, x], axis=0), me + 1, others, axis=0)

    pair_slots = from_me(contact_slots[0, 0]).reshape(1, -1)
    live = from_me(contact_live[0, 0]).reshape(1, -1)
    c_block = jnp.where(live > 0, pair_slots // block_slots, -1)
    c_index = pair_slots % block_slots
    ghost = jnp.concatenate([left_ghost[0, 0], right_ghost[0, 0]])[None]
    pairs = contact_slots.shape[3]
    ghosts = left_ghost.shape[2]

    u, p = pl.pallas_call(
        functools.partial(step_kernel, others, segments, 512),
        out_shape=[jax.ShapeDtypeStruct((rows, wide), f32)] * 2,
        in_specs=[vmem] * 8,
        out_specs=[vmem] * 2,
        scratch_shapes=[
            pltpu.VMEM((wide, others * pairs), bf16),
            pltpu.VMEM((wide, 2 * ghosts), bf16),
            pltpu.VMEM((rows, wide), f32),
            pltpu.VMEM((others, SUB, pairs // 2), f32),
            pltpu.VMEM((ITERS, others, SUB, pairs // 2), f32),
            pltpu.VMEM((2, SUB, ghosts // 2), f32),
            pltpu.VMEM((ITERS, 2, SUB, ghosts // 2), f32),
            pltpu.SemaphoreType.DMA((others,)),
            pltpu.SemaphoreType.DMA((ITERS, others)),
            pltpu.SemaphoreType.DMA((2,)),
            pltpu.SemaphoreType.DMA((ITERS, 2)),
        ],
        compiler_params=pltpu.CompilerParams(
            collective_id=0, has_side_effects=True, vmem_limit_bytes=48 * 1024 * 1024
        ),
        name="steps",
    )(u, p, mass, operators, c_block, c_index, ghost // block_slots, ghost % block_slots)

    def unlay(x):
        x = x.reshape(blocks, SUB, wide)[:, :parts, :block_slots]
        return x.transpose(1, 0, 2).reshape(1, 1, parts, slots)

    return unlay(u), unlay(p)


def solution(mesh):
    four = P("len", "wire", None, None)
    three = P("len", "wire", None)
    return jax.shard_map(
        on_device,
        mesh=mesh,
        in_specs=(four, four, four, three, P(), three, three, three, four, four),
        out_specs=(four, four),
        check_vma=False,
    )
```

```python
import functools

import jax
import jax.numpy as jnp
from jax import lax
from jax.experimental import pallas as pl
from jax.experimental.pallas import tpu as pltpu
from jax.sharding import PartitionSpec as P

ITERS = 4
PENALTY = 4.0
TIME_SQUARE = 0.03
block_slots = 224
block_elements = 4
LANES = 128
BLOCK_SCALE, BLOCK_SHIFT = 4682, 20
SUB = 8
f32 = jnp.float32
bf16 = jnp.bfloat16
MESH = pl.DeviceIdType.MESH


def round_up(value, step):
    return -(-value // step) * step


def dot(a, b):
    return jnp.dot(a, b, preferred_element_type=f32)


def dot_nt(a, b):
    return lax.dot_general(a, b, (((1,), (1,)), ((), ())), preferred_element_type=f32)


def step_kernel(
    wires,
    segments,
    chunk,
    u_in, p_in, nodes_in, stiff_in, grad_in, mass_in, left_in, right_in, slots_in, live_in,
    u_out, p_out,
    u_ref, p_ref, mass_ref,
    c_hot, g_hot, e_hot, cb_ref, gb_ref, gram, nodes_ref, stiff_ref,
    part, picked, c_send, c_recv, g_send, g_recv,
    c_ssem, c_rsem, g_ssem, g_rsem,
):
    others = wires - 1
    blocks = e_hot.shape[0]
    parts = u_in.shape[1]
    rows, wide = u_ref.shape
    pairs = slots_in.shape[3]
    ghosts = left_in.shape[2]
    elements, node_count = nodes_in.shape[2:]
    node_pad = gram.shape[0]
    me = lax.axis_index("wire")
    seg = lax.axis_index("len")
    has_prev = seg > 0
    has_next = seg < segments - 1
    mirrored = wires & (wires - 1) == 0

    def partner(d):
        if not mirrored:
            return lax.rem(me + (d + 1), wires)
        offset, other, bit = wires - 1 - d, me, 1
        while bit <= offset:
            if offset & bit:
                other = other + bit - 2 * bit * lax.rem(lax.div(me, bit), 2)
            bit *= 2
        return other

    def landing(d):
        return d if mirrored else others - 1 - d

    barrier = pltpu.get_barrier_semaphore()
    for d in range(others):
        pl.semaphore_signal(barrier, inc=1, device_id={"wire": partner(d)}, device_id_type=MESH)

    @pl.when(has_prev)
    def _():
        pl.semaphore_signal(barrier, inc=1, device_id={"len": seg - 1}, device_id_type=MESH)

    @pl.when(has_next)
    def _():
        pl.semaphore_signal(barrier, inc=1, device_id={"len": seg + 1}, device_id_type=MESH)

    def block_of(slots):
        return (slots * BLOCK_SCALE) >> BLOCK_SHIFT

    def fill(hot, base_ref, at, slots, live):
        count = slots.shape[1]
        which = block_of(slots)
        inside = slots - which * block_slots
        if live is not None:
            which = jnp.where(live > 0, which, -1)
        base_ref[:, at : at + count] = jnp.broadcast_to(which, (SUB, count))
        for start in range(0, count, LANES):
            ids = lax.broadcasted_iota(jnp.int32, (wide, LANES), 0)
            here = inside[:, start : start + LANES]
            hot[:, at + start : at + start + LANES] = jnp.where(ids == here, 1.0, 0.0).astype(bf16)

    u_ref[...] = jnp.zeros_like(u_ref)
    p_ref[...] = jnp.zeros_like(p_ref)
    for b in range(blocks):
        lanes = slice(b * block_slots, (b + 1) * block_slots)
        for c in range(parts):
            row = slice(b * SUB + c, b * SUB + c + 1)
            u_ref[row, :block_slots] = u_in[0, c, :, lanes]
            p_ref[row, :block_slots] = p_in[0, c, :, lanes]
    for d in range(others):
        fill(c_hot, cb_ref, d * pairs, slots_in[0, 0, pl.ds(partner(d), 1), :], live_in[0, 0, pl.ds(partner(d), 1), :])

    @pl.when(jnp.logical_not(has_prev))
    def _():
        g_recv[:, 0] = jnp.zeros((ITERS,) + g_recv.shape[2:], f32)

    @pl.when(jnp.logical_not(has_next))
    def _():
        g_recv[:, 1] = jnp.zeros((ITERS,) + g_recv.shape[2:], f32)

    def prepare():
        row8 = lax.broadcasted_iota(jnp.int32, (SUB, wide), 0)
        lane8 = lax.broadcasted_iota(jnp.int32, (SUB, wide), 1)
        for b in range(blocks):
            at = slice(b * SUB, (b + 1) * SUB)
            lanes = slice(b * block_slots, (b + 1) * block_slots)
            mass_ref[at, :] = jnp.where((row8 == 3) & (lane8 >= block_slots), 1.0, 0.0)
            mass_ref[b * SUB + 3 : b * SUB + 4, :block_slots] = mass_in[0, :, lanes]
        fill(g_hot, gb_ref, 0, left_in[0], None)
        fill(g_hot, gb_ref, ghosts, right_in[0], None)
        op = grad_in[...]
        product = lax.dot_general(
            op, op, (((0,), (0,)), ((), ())), precision=lax.Precision.HIGHEST, preferred_element_type=f32
        )
        high = product.astype(bf16)
        gram[...] = jnp.zeros_like(gram)
        gram[:node_count, :node_count] = high
        gram[:node_count, node_pad : node_pad + node_count] = (product - high.astype(f32)).astype(bf16)
        nodes_ref[...] = jnp.full(nodes_ref.shape, -1, jnp.int32)
        nodes_ref[:, :node_count] = nodes_in[0, 0]
        stiff_ref[...] = jnp.zeros_like(stiff_ref)
        stiff_ref[:, :elements] = jnp.broadcast_to(stiff_in[0], (stiff_ref.shape[0], elements))
        stiff_ref[...] = jnp.transpose(stiff_ref[...])
        for b in range(blocks):
            for e in range(block_elements):
                one = b * block_elements + e
                ids = lax.broadcasted_iota(jnp.int32, (wide, node_pad), 0)
                hot = jnp.where(ids == nodes_ref[one : one + 1, :], 1.0, 0.0).astype(bf16)
                e_hot[b, :, e * node_pad : (e + 1) * node_pad] = hot

    last = segments - 1
    pl.semaphore_wait(
        barrier, others + lax.div(seg + last, segments) + lax.div(last - seg + last, segments)
    )

    row_all = lax.broadcasted_iota(jnp.int32, (rows, wide), 0) & (SUB - 1)
    low_all = row_all < 4

    def rows_of(width):
        return lax.broadcasted_iota(jnp.int32, (SUB, width), 0)

    def split(x):
        high = x.astype(bf16).astype(f32)
        return jnp.where(low_all, high, pltpu.roll(x - high, 4, 0)).astype(bf16)

    def take(packed, hot, base_ref, start, width):
        cols = slice(start, start + width)
        picked = dot(packed, hot[:, cols])
        which = base_ref[:, cols]
        total = jnp.zeros((SUB, width), f32)
        for b in range(blocks):
            total = jnp.where(which == b, picked[b * SUB : (b + 1) * SUB], total)
        return total + pltpu.roll(total, 4, 0)

    def put(values, hot, base_ref, start, width):
        cols = slice(start, start + width)
        high = values.astype(bf16).astype(f32)
        values = jnp.where(rows_of(width) < 4, high, values - high)
        which = base_ref[:, cols]
        spread = jnp.concatenate([jnp.where(which == b, values, 0.0) for b in range(blocks)], axis=0)
        return dot_nt(spread.astype(bf16), hot[:, cols])

    def take_list(packed, hot, base_ref, start, count, out_ref):
        half = count // 2
        width = chunk if half % chunk == 0 else half
        for at in range(0, half, width):
            first = take(packed, hot, base_ref, start + at, width)
            second = take(packed, hot, base_ref, start + half + at, width)
            out_ref[:, at : at + width] = jnp.where(rows_of(width) < 4, first, second)

    def put_list(values, hot, base_ref, start, count, total):
        half = count // 2
        width = chunk if half % chunk == 0 else half
        for at in range(0, half, width):
            here = values[:, at : at + width]
            turned = pltpu.roll(here, 4, 0)
            low = rows_of(width) < 4
            total = total + put(jnp.where(low, here, turned), hot, base_ref, start + at, width)
            total = total + put(jnp.where(low, turned, here), hot, base_ref, start + half + at, width)
        return total

    def contact_copy(step, d):
        return pltpu.make_async_remote_copy(
            src_ref=c_send.at[d],
            dst_ref=c_recv.at[step, landing(d)],
            send_sem=c_ssem.at[d],
            recv_sem=c_rsem.at[step, landing(d)],
            device_id={"wire": partner(d)},
            device_id_type=MESH,
        )

    def contact_arrival(step, d):
        return pltpu.make_async_remote_copy(
            src_ref=c_send.at[d],
            dst_ref=c_recv.at[step, d],
            send_sem=c_ssem.at[d],
            recv_sem=c_rsem.at[step, d],
            device_id={"wire": partner(d)},
            device_id_type=MESH,
        )

    def ghost_copy(step, side):
        return pltpu.make_async_remote_copy(
            src_ref=g_send.at[side],
            dst_ref=g_recv.at[step, 1 - side],
            send_sem=g_ssem.at[side],
            recv_sem=g_rsem.at[step, 1 - side],
            device_id={"len": seg - 1 if side == 0 else seg + 1},
            device_id_type=MESH,
        )

    def ghost_arrival(step, side):
        return pltpu.make_async_remote_copy(
            src_ref=g_send.at[side],
            dst_ref=g_recv.at[step, side],
            send_sem=g_ssem.at[side],
            recv_sem=g_rsem.at[step, side],
            device_id={"len": seg - 1 if side == 0 else seg + 1},
            device_id_type=MESH,
        )

    exists = (has_prev, has_next)

    def one_step(step, _):
        packed = split(u_ref[...])
        for d in range(others):
            take_list(packed, c_hot, cb_ref, d * pairs, pairs, c_send.at[d])
            contact_copy(step, d).start()

        @pl.when(step == 0)
        def _():
            prepare()

        both = 2 * SUB
        for b in range(blocks):
            pair = packed[(b // 2) * both : (b // 2 + 1) * both]
            out = dot(pair, e_hot[b])[(b % 2) * SUB : (b % 2 + 1) * SUB]
            for e in range(block_elements):
                one = b * block_elements + e
                picked[one * SUB : (one + 1) * SUB, :] = out[:, e * node_pad : (e + 1) * node_pad]
        reach = elements * SUB // 4
        for at in range(0, elements * SUB, reach):
            out = dot(picked[at : at + reach, :].astype(bf16), gram[...])
            main = out[:, :node_pad]
            main = main + pltpu.roll(main, reach - 4, 0) + out[:, node_pad:]
            for i in range(0, reach, SUB):
                one = (at + i) // SUB
                r = main[i : i + SUB] * jnp.broadcast_to(stiff_ref[one : one + 1, :], (SUB, node_pad))
                high = r.astype(bf16).astype(f32)
                low = jnp.where(rows_of(node_pad) < 4, high, pltpu.roll(r - high, 4, 0))
                picked[at + i : at + i + SUB, :] = low
        for b in range(0, blocks, 2):
            pair = jnp.concatenate(
                [
                    jnp.concatenate(
                        [
                            picked[one * SUB : (one + 1) * SUB, :]
                            for one in range(k * block_elements, (k + 1) * block_elements)
                        ],
                        axis=1,
                    )
                    for k in (b, b + 1)
                ],
                axis=0,
            ).astype(bf16)
            for k in range(2):
                out = dot_nt(pair, e_hot[b + k])[k * SUB : (k + 1) * SUB]
                part[(b + k) * SUB : (b + k + 1) * SUB, :] = out + pltpu.roll(out, 4, 0)

        spread = jnp.zeros((rows, wide), f32)
        for d in reversed(range(others)):
            contact_arrival(step, d).wait_recv()
            spread = put_list(c_recv[step, d] - c_send[d], c_hot, cb_ref, d * pairs, pairs, spread)
        spread = spread + pltpu.roll(spread, rows - 4, 0)
        local = jnp.where(row_all < 3, PENALTY * spread - part[...], mass_ref[...])
        part[...] = local

        packed = split(local)
        for side in range(2):
            take_list(packed, g_hot, gb_ref, side * ghosts, ghosts, g_send.at[side])

            @pl.when(exists[side])
            def _():
                ghost_copy(step, side).start()

        spread = jnp.zeros((rows, wide), f32)
        for side in range(2):

            @pl.when(exists[side])
            def _():
                ghost_arrival(step, side).wait_recv()

            spread = put_list(g_recv[step, side], g_hot, gb_ref, side * ghosts, ghosts, spread)
        spread = spread + pltpu.roll(spread, rows - 4, 0)
        total = jnp.where(low_all, part[...] + spread, 0.0)
        for b in range(blocks):
            at = slice(b * SUB, (b + 1) * SUB)
            force = total[at]
            mass = jnp.broadcast_to(force[3:4], force.shape)
            now = u_ref[at, :]
            stepped = 2.0 * now - p_ref[at, :] + TIME_SQUARE * force / mass
            p_ref[at, :] = now
            u_ref[at, :] = jnp.where(rows_of(wide) < 3, stepped, 0.0)

        for d in range(others):
            contact_copy(step, d).wait_send()
        for side in range(2):

            @pl.when(exists[side])
            def _():
                ghost_copy(step, side).wait_send()

        return 0

    lax.fori_loop(0, ITERS, one_step, 0)
    for b in range(blocks):
        lanes = slice(b * block_slots, (b + 1) * block_slots)
        for c in range(parts):
            row = slice(b * SUB + c, b * SUB + c + 1)
            u_out[0, c, :, lanes] = u_ref[row, :block_slots]
            p_out[0, c, :, lanes] = p_ref[row, :block_slots]


def on_device(displacement, previous, element_nodes, *rest):
    left_ghost, contact_slots = rest[3], rest[5]
    node_count, elements = element_nodes.shape[2:]
    blocks = elements // block_elements
    wide = round_up(block_slots, 2 * LANES)
    node_pad = round_up(node_count, LANES)
    wires = lax.axis_size("wire")
    others = wires - 1
    rows = blocks * SUB
    pairs = contact_slots.shape[3]
    ghosts = left_ghost.shape[2]
    assert blocks % 2 == 0 and elements <= LANES and node_pad == LANES
    assert all((x * BLOCK_SCALE) >> BLOCK_SHIFT == x // block_slots for x in range(blocks * block_slots))

    vmem = pl.BlockSpec(memory_space=pltpu.VMEM)
    turned = jnp.swapaxes(displacement, 1, 2)
    args = (turned, jnp.swapaxes(previous, 1, 2), jnp.swapaxes(element_nodes, 2, 3), *rest)
    results = pl.pallas_call(
        functools.partial(step_kernel, wires, lax.axis_size("len"), 512),
        out_shape=[jax.ShapeDtypeStruct(turned.shape, f32)] * 2,
        in_specs=[vmem] * len(args),
        out_specs=[vmem] * 2,
        scratch_shapes=[
            pltpu.VMEM((rows, wide), f32),
            pltpu.VMEM((rows, wide), f32),
            pltpu.VMEM((rows, wide), f32),
            pltpu.VMEM((wide, others * pairs), bf16),
            pltpu.VMEM((wide, 2 * ghosts), bf16),
            pltpu.VMEM((blocks, wide, block_elements * node_pad), bf16),
            pltpu.VMEM((SUB, others * pairs), jnp.int32),
            pltpu.VMEM((SUB, 2 * ghosts), jnp.int32),
            pltpu.VMEM((node_pad, 2 * node_pad), bf16),
            pltpu.VMEM((elements, node_pad), jnp.int32),
            pltpu.VMEM((LANES, LANES), f32),
            pltpu.VMEM((rows, wide), f32),
            pltpu.VMEM((elements * SUB, node_pad), f32),
            pltpu.VMEM((others, SUB, pairs // 2), f32),
            pltpu.VMEM((ITERS, others, SUB, pairs // 2), f32),
            pltpu.VMEM((2, SUB, ghosts // 2), f32),
            pltpu.VMEM((ITERS, 2, SUB, ghosts // 2), f32),
            pltpu.SemaphoreType.DMA((others,)),
            pltpu.SemaphoreType.DMA((ITERS, others)),
            pltpu.SemaphoreType.DMA((2,)),
            pltpu.SemaphoreType.DMA((ITERS, 2)),
        ],
        compiler_params=pltpu.CompilerParams(
            collective_id=0, has_side_effects=True, vmem_limit_bytes=48 * 1024 * 1024
        ),
        name="steps",
    )(*args)
    return tuple(jnp.swapaxes(x, 1, 2) for x in results)


def solution(mesh):
    four = P("len", "wire", None, None)
    three = P("len", "wire", None)
    return jax.shard_map(
        on_device,
        mesh=mesh,
        in_specs=(four, four, four, three, P(), three, three, three, four, four),
        out_specs=(four, four),
        check_vma=False,
    )
```

```python
import functools

import jax
import jax.numpy as jnp
from jax import lax
from jax.experimental import pallas as pl
from jax.experimental.pallas import tpu as pltpu
from jax.sharding import PartitionSpec as P

ITERS = 4
PENALTY = 4.0
TIME_SQUARE = 0.03
block_slots = 224
block_elements = 4
LANES = 128
ARGS = 10
VMEM_BYTES = 67_043_328
FIRST = (8, 9, 0)
LATER = (1, 2, 3, 4, 5, 6, 7)
BLOCK_SCALE, BLOCK_SHIFT = 4682, 20
SUB = 8
f32 = jnp.float32
bf16 = jnp.bfloat16
MESH = pl.DeviceIdType.MESH


def round_up(value, step):
    return -(-value // step) * step


def dot(a, b):
    return jnp.dot(a, b, preferred_element_type=f32)


def dot_nt(a, b):
    return lax.dot_general(a, b, (((1,), (1,)), ((), ())), preferred_element_type=f32)


def step_kernel(
    wires,
    segments,
    chunk,
    *refs,
):
    sources, refs = refs[:ARGS], refs[ARGS:]
    inputs, in_sem, refs = refs[2 : 2 + ARGS], refs[2 + ARGS], refs[:2] + refs[3 + ARGS :]
    copies = [
        pltpu.make_async_copy(source, target, in_sem.at[i])
        for i, (source, target) in enumerate(zip(sources, inputs))
    ]
    for i in FIRST + LATER:
        copies[i].start()
    run(wires, segments, chunk, copies, *inputs, *refs)


def run(
    wires,
    segments,
    chunk,
    copies,
    u_in, p_in, nodes_in, stiff_in, grad_in, mass_in, left_in, right_in, slots_in, live_in,
    u_out, p_out,
    u_ref, p_ref, mass_ref,
    c_hot, g_hot, e_hot, cb_ref, gb_ref, gram, nodes_ref, stiff_ref,
    part, picked, c_send, c_recv, g_send, g_recv,
    c_ssem, c_rsem, g_ssem, g_rsem,
):
    others = wires - 1
    blocks = e_hot.shape[0]
    parts = u_in.shape[1]
    rows, wide = u_ref.shape
    pairs = slots_in.shape[3]
    ghosts = left_in.shape[2]
    elements, node_count = nodes_in.shape[2:]
    node_pad = gram.shape[0]
    me = lax.axis_index("wire")
    seg = lax.axis_index("len")
    has_prev = seg > 0
    has_next = seg < segments - 1
    mirrored = wires & (wires - 1) == 0

    def partner(d):
        if not mirrored:
            return lax.rem(me + (d + 1), wires)
        offset, other, bit = wires - 1 - d, me, 1
        while bit <= offset:
            if offset & bit:
                other = other + bit - 2 * bit * lax.rem(lax.div(me, bit), 2)
            bit *= 2
        return other

    def landing(d):
        return d if mirrored else others - 1 - d

    barrier = pltpu.get_barrier_semaphore()
    for d in range(others):
        pl.semaphore_signal(barrier, inc=1, device_id={"wire": partner(d)}, device_id_type=MESH)

    @pl.when(has_prev)
    def _():
        pl.semaphore_signal(barrier, inc=1, device_id={"len": seg - 1}, device_id_type=MESH)

    @pl.when(has_next)
    def _():
        pl.semaphore_signal(barrier, inc=1, device_id={"len": seg + 1}, device_id_type=MESH)

    def block_of(slots):
        return (slots * BLOCK_SCALE) >> BLOCK_SHIFT

    def fill(hot, base_ref, at, slots, live):
        count = slots.shape[1]
        which = block_of(slots)
        inside = slots - which * block_slots
        if live is not None:
            which = jnp.where(live > 0, which, -1)
        base_ref[:, at : at + count] = jnp.broadcast_to(which, (SUB, count))
        for start in range(0, count, LANES):
            ids = lax.broadcasted_iota(jnp.int32, (wide, LANES), 0)
            here = inside[:, start : start + LANES]
            hot[:, at + start : at + start + LANES] = jnp.where(ids == here, 1.0, 0.0).astype(bf16)

    for i in FIRST:
        copies[i].wait()
    u_ref[...] = jnp.zeros_like(u_ref)
    p_ref[...] = jnp.zeros_like(p_ref)
    for b in range(blocks):
        lanes = slice(b * block_slots, (b + 1) * block_slots)
        for c in range(parts):
            row = slice(b * SUB + c, b * SUB + c + 1)
            u_ref[row, :block_slots] = u_in[0, c, :, lanes]
    for d in range(others):
        fill(c_hot, cb_ref, d * pairs, slots_in[0, 0, pl.ds(partner(d), 1), :], live_in[0, 0, pl.ds(partner(d), 1), :])

    @pl.when(jnp.logical_not(has_prev))
    def _():
        g_recv[:, 0] = jnp.zeros((ITERS,) + g_recv.shape[2:], f32)

    @pl.when(jnp.logical_not(has_next))
    def _():
        g_recv[:, 1] = jnp.zeros((ITERS,) + g_recv.shape[2:], f32)

    def prepare():
        for i in LATER:
            copies[i].wait()
        row8 = lax.broadcasted_iota(jnp.int32, (SUB, wide), 0)
        lane8 = lax.broadcasted_iota(jnp.int32, (SUB, wide), 1)
        for b in range(blocks):
            at = slice(b * SUB, (b + 1) * SUB)
            lanes = slice(b * block_slots, (b + 1) * block_slots)
            mass_ref[at, :] = jnp.where((row8 == 3) & (lane8 >= block_slots), 1.0, 0.0)
            for c in range(parts):
                p_ref[b * SUB + c : b * SUB + c + 1, :block_slots] = p_in[0, c, :, lanes]
            mass_ref[b * SUB + 3 : b * SUB + 4, :block_slots] = mass_in[0, :, lanes]
        fill(g_hot, gb_ref, 0, left_in[0], None)
        fill(g_hot, gb_ref, ghosts, right_in[0], None)
        op = grad_in[...]
        product = lax.dot_general(
            op, op, (((0,), (0,)), ((), ())), precision=lax.Precision.HIGHEST, preferred_element_type=f32
        )
        high = product.astype(bf16)
        gram[...] = jnp.zeros_like(gram)
        gram[:node_count, :node_count] = high
        gram[:node_count, node_pad : node_pad + node_count] = (product - high.astype(f32)).astype(bf16)
        nodes_ref[...] = jnp.full(nodes_ref.shape, -1, jnp.int32)
        nodes_ref[:, :node_count] = nodes_in[0, 0]
        stiff_ref[...] = jnp.zeros_like(stiff_ref)
        stiff_ref[:, :elements] = jnp.broadcast_to(stiff_in[0], (stiff_ref.shape[0], elements))
        stiff_ref[...] = jnp.transpose(stiff_ref[...])
        for b in range(blocks):
            for e in range(block_elements):
                one = b * block_elements + e
                ids = lax.broadcasted_iota(jnp.int32, (wide, node_pad), 0)
                hot = jnp.where(ids == nodes_ref[one : one + 1, :], 1.0, 0.0).astype(bf16)
                e_hot[b, :, e * node_pad : (e + 1) * node_pad] = hot

    last = segments - 1
    pl.semaphore_wait(
        barrier, others + lax.div(seg + last, segments) + lax.div(last - seg + last, segments)
    )

    row_all = lax.broadcasted_iota(jnp.int32, (rows, wide), 0) & (SUB - 1)
    low_all = row_all < 4

    def rows_of(width):
        return lax.broadcasted_iota(jnp.int32, (SUB, width), 0)

    def split(x):
        high = x.astype(bf16).astype(f32)
        return jnp.where(low_all, high, pltpu.roll(x - high, 4, 0)).astype(bf16)

    def take(packed, hot, base_ref, start, width):
        cols = slice(start, start + width)
        picked = dot(packed, hot[:, cols])
        which = base_ref[:, cols]
        total = jnp.zeros((SUB, width), f32)
        for b in range(blocks):
            total = jnp.where(which == b, picked[b * SUB : (b + 1) * SUB], total)
        return total + pltpu.roll(total, 4, 0)

    def put(values, hot, base_ref, start, width):
        cols = slice(start, start + width)
        high = values.astype(bf16).astype(f32)
        values = jnp.where(rows_of(width) < 4, high, values - high)
        which = base_ref[:, cols]
        spread = jnp.concatenate([jnp.where(which == b, values, 0.0) for b in range(blocks)], axis=0)
        return dot_nt(spread.astype(bf16), hot[:, cols])

    def take_list(packed, hot, base_ref, start, count, out_ref):
        half = count // 2
        width = chunk if half % chunk == 0 else half
        for at in range(0, half, width):
            first = take(packed, hot, base_ref, start + at, width)
            second = take(packed, hot, base_ref, start + half + at, width)
            out_ref[:, at : at + width] = jnp.where(rows_of(width) < 4, first, second)

    def put_list(values, hot, base_ref, start, count, total):
        half = count // 2
        width = chunk if half % chunk == 0 else half
        for at in range(0, half, width):
            here = values[:, at : at + width]
            turned = pltpu.roll(here, 4, 0)
            low = rows_of(width) < 4
            total = total + put(jnp.where(low, here, turned), hot, base_ref, start + at, width)
            total = total + put(jnp.where(low, turned, here), hot, base_ref, start + half + at, width)
        return total

    def contact_copy(step, d):
        return pltpu.make_async_remote_copy(
            src_ref=c_send.at[d],
            dst_ref=c_recv.at[step, landing(d)],
            send_sem=c_ssem.at[d],
            recv_sem=c_rsem.at[step, landing(d)],
            device_id={"wire": partner(d)},
            device_id_type=MESH,
        )

    def contact_arrival(step, d):
        return pltpu.make_async_remote_copy(
            src_ref=c_send.at[d],
            dst_ref=c_recv.at[step, d],
            send_sem=c_ssem.at[d],
            recv_sem=c_rsem.at[step, d],
            device_id={"wire": partner(d)},
            device_id_type=MESH,
        )

    def ghost_copy(step, side):
        return pltpu.make_async_remote_copy(
            src_ref=g_send.at[side],
            dst_ref=g_recv.at[step, 1 - side],
            send_sem=g_ssem.at[side],
            recv_sem=g_rsem.at[step, 1 - side],
            device_id={"len": seg - 1 if side == 0 else seg + 1},
            device_id_type=MESH,
        )

    def ghost_arrival(step, side):
        return pltpu.make_async_remote_copy(
            src_ref=g_send.at[side],
            dst_ref=g_recv.at[step, side],
            send_sem=g_ssem.at[side],
            recv_sem=g_rsem.at[step, side],
            device_id={"len": seg - 1 if side == 0 else seg + 1},
            device_id_type=MESH,
        )

    exists = (has_prev, has_next)

    def one_step(step, _):
        packed = split(u_ref[...])
        for d in range(others):
            take_list(packed, c_hot, cb_ref, d * pairs, pairs, c_send.at[d])
            contact_copy(step, d).start()

        @pl.when(step == 0)
        def _():
            prepare()

        both = 2 * SUB
        for b in range(blocks):
            pair = packed[(b // 2) * both : (b // 2 + 1) * both]
            out = dot(pair, e_hot[b])[(b % 2) * SUB : (b % 2 + 1) * SUB]
            for e in range(block_elements):
                one = b * block_elements + e
                picked[one * SUB : (one + 1) * SUB, :] = out[:, e * node_pad : (e + 1) * node_pad]
        reach = elements * SUB // 4
        for at in range(0, elements * SUB, reach):
            out = dot(picked[at : at + reach, :].astype(bf16), gram[...])
            main = out[:, :node_pad]
            main = main + pltpu.roll(main, reach - 4, 0) + out[:, node_pad:]
            for i in range(0, reach, SUB):
                one = (at + i) // SUB
                r = main[i : i + SUB] * jnp.broadcast_to(stiff_ref[one : one + 1, :], (SUB, node_pad))
                high = r.astype(bf16).astype(f32)
                low = jnp.where(rows_of(node_pad) < 4, high, pltpu.roll(r - high, 4, 0))
                picked[at + i : at + i + SUB, :] = low
        for b in range(0, blocks, 2):
            pair = jnp.concatenate(
                [
                    jnp.concatenate(
                        [
                            picked[one * SUB : (one + 1) * SUB, :]
                            for one in range(k * block_elements, (k + 1) * block_elements)
                        ],
                        axis=1,
                    )
                    for k in (b, b + 1)
                ],
                axis=0,
            ).astype(bf16)
            for k in range(2):
                out = dot_nt(pair, e_hot[b + k])[k * SUB : (k + 1) * SUB]
                part[(b + k) * SUB : (b + k + 1) * SUB, :] = out + pltpu.roll(out, 4, 0)

        spread = jnp.zeros((rows, wide), f32)
        for d in reversed(range(others)):
            contact_arrival(step, d).wait_recv()
            spread = put_list(c_recv[step, d] - c_send[d], c_hot, cb_ref, d * pairs, pairs, spread)
        spread = spread + pltpu.roll(spread, rows - 4, 0)
        local = jnp.where(row_all < 3, PENALTY * spread - part[...], mass_ref[...])
        part[...] = local

        packed = split(local)
        for side in range(2):
            take_list(packed, g_hot, gb_ref, side * ghosts, ghosts, g_send.at[side])

            @pl.when(exists[side])
            def _():
                ghost_copy(step, side).start()

        spread = jnp.zeros((rows, wide), f32)
        for side in range(2):

            @pl.when(exists[side])
            def _():
                ghost_arrival(step, side).wait_recv()

            spread = put_list(g_recv[step, side], g_hot, gb_ref, side * ghosts, ghosts, spread)
        spread = spread + pltpu.roll(spread, rows - 4, 0)
        total = jnp.where(low_all, part[...] + spread, 0.0)
        for b in range(blocks):
            at = slice(b * SUB, (b + 1) * SUB)
            force = total[at]
            mass = jnp.broadcast_to(force[3:4], force.shape)
            now = u_ref[at, :]
            stepped = 2.0 * now - p_ref[at, :] + TIME_SQUARE * force / mass
            p_ref[at, :] = now
            u_ref[at, :] = jnp.where(rows_of(wide) < 3, stepped, 0.0)

        for d in range(others):
            contact_copy(step, d).wait_send()
        for side in range(2):

            @pl.when(exists[side])
            def _():
                ghost_copy(step, side).wait_send()

        return 0

    lax.fori_loop(0, ITERS, one_step, 0)
    for b in range(blocks):
        lanes = slice(b * block_slots, (b + 1) * block_slots)
        for c in range(parts):
            row = slice(b * SUB + c, b * SUB + c + 1)
            u_out[0, c, :, lanes] = u_ref[row, :block_slots]
            p_out[0, c, :, lanes] = p_ref[row, :block_slots]


def on_device(displacement, previous, element_nodes, *rest):
    left_ghost, contact_slots = rest[3], rest[5]
    node_count, elements = element_nodes.shape[2:]
    blocks = elements // block_elements
    wide = round_up(block_slots, 2 * LANES)
    node_pad = round_up(node_count, LANES)
    wires = lax.axis_size("wire")
    others = wires - 1
    rows = blocks * SUB
    pairs = contact_slots.shape[3]
    ghosts = left_ghost.shape[2]
    assert blocks % 2 == 0 and elements <= LANES and node_pad == LANES
    assert all((x * BLOCK_SCALE) >> BLOCK_SHIFT == x // block_slots for x in range(blocks * block_slots))

    vmem = pl.BlockSpec(memory_space=pltpu.VMEM)
    turned = jnp.swapaxes(displacement, 1, 2)
    args = (turned, jnp.swapaxes(previous, 1, 2), jnp.swapaxes(element_nodes, 2, 3), *rest)
    results = pl.pallas_call(
        functools.partial(step_kernel, wires, lax.axis_size("len"), 512),
        out_shape=[jax.ShapeDtypeStruct(turned.shape, f32)] * 2,
        in_specs=[pl.BlockSpec(memory_space=pl.ANY)] * len(args),
        out_specs=[vmem] * 2,
        scratch_shapes=[pltpu.VMEM(x.shape, x.dtype) for x in args]
        + [pltpu.SemaphoreType.DMA((len(args),))]
        + [
            pltpu.VMEM((rows, wide), f32),
            pltpu.VMEM((rows, wide), f32),
            pltpu.VMEM((rows, wide), f32),
            pltpu.VMEM((wide, others * pairs), bf16),
            pltpu.VMEM((wide, 2 * ghosts), bf16),
            pltpu.VMEM((blocks, wide, block_elements * node_pad), bf16),
            pltpu.VMEM((SUB, others * pairs), jnp.int32),
            pltpu.VMEM((SUB, 2 * ghosts), jnp.int32),
            pltpu.VMEM((node_pad, 2 * node_pad), bf16),
            pltpu.VMEM((elements, node_pad), jnp.int32),
            pltpu.VMEM((LANES, LANES), f32),
            pltpu.VMEM((rows, wide), f32),
            pltpu.VMEM((elements * SUB, node_pad), f32),
            pltpu.VMEM((others, SUB, pairs // 2), f32),
            pltpu.VMEM((ITERS, others, SUB, pairs // 2), f32),
            pltpu.VMEM((2, SUB, ghosts // 2), f32),
            pltpu.VMEM((ITERS, 2, SUB, ghosts // 2), f32),
            pltpu.SemaphoreType.DMA((others,)),
            pltpu.SemaphoreType.DMA((ITERS, others)),
            pltpu.SemaphoreType.DMA((2,)),
            pltpu.SemaphoreType.DMA((ITERS, 2)),
        ],
        compiler_params=pltpu.CompilerParams(
            collective_id=0, has_side_effects=True, vmem_limit_bytes=VMEM_BYTES
        ),
        name="steps",
    )(*args)
    return tuple(jnp.swapaxes(x, 1, 2) for x in results)


def solution(mesh):
    four = P("len", "wire", None, None)
    three = P("len", "wire", None)
    return jax.shard_map(
        on_device,
        mesh=mesh,
        in_specs=(four, four, four, three, P(), three, three, three, four, four),
        out_specs=(four, four),
        check_vma=False,
    )
```

```python
import functools

import jax
import jax.numpy as jnp
from jax import lax
from jax.experimental import pallas as pl
from jax.experimental.pallas import tpu as pltpu
from jax.sharding import PartitionSpec as P

ITERS = 4
PENALTY = 4.0
TIME_SQUARE = 0.03
block_slots = 224
block_elements = 4
LANES = 128
ARGS = 10
VMEM_BYTES = 67_043_328
FIRST = (8, 9, 0)
LATER = (1, 2, 3, 4, 5, 6, 7)
BLOCK_SCALE, BLOCK_SHIFT = 4682, 20
SUB = 8
f32 = jnp.float32
bf16 = jnp.bfloat16
MESH = pl.DeviceIdType.MESH


def round_up(value, step):
    return -(-value // step) * step


def dot(a, b):
    return jnp.dot(a, b, preferred_element_type=f32)


def dot_nt(a, b):
    return lax.dot_general(a, b, (((1,), (1,)), ((), ())), preferred_element_type=f32)


def step_kernel(
    wires,
    segments,
    chunk,
    *refs,
):
    sources, refs = refs[:ARGS], refs[ARGS:]
    inputs, in_sem, refs = refs[2 : 2 + ARGS], refs[2 + ARGS], refs[:2] + refs[3 + ARGS :]
    copies = [
        pltpu.make_async_copy(source, target, in_sem.at[i])
        for i, (source, target) in enumerate(zip(sources, inputs))
    ]
    for i in FIRST + LATER:
        copies[i].start()
    run(wires, segments, chunk, copies, *inputs, *refs)


def run(
    wires,
    segments,
    chunk,
    copies,
    u_in, p_in, nodes_in, stiff_in, grad_in, mass_in, left_in, right_in, slots_in, live_in,
    u_out, p_out,
    u_ref, p_ref, mass_ref,
    c_hot, g_hot, e_hot, cb_ref, gb_ref, gram, nodes_ref, stiff_ref,
    part, picked, c_send, c_recv, g_send, g_recv,
    c_ssem, c_rsem, g_ssem, g_rsem,
):
    others = wires - 1
    blocks = e_hot.shape[0]
    parts = u_in.shape[1]
    rows, wide = u_ref.shape
    pairs = slots_in.shape[3]
    ghosts = left_in.shape[2]
    elements, node_count = nodes_in.shape[2:]
    node_pad = gram.shape[0]
    me = lax.axis_index("wire")
    seg = lax.axis_index("len")
    has_prev = seg > 0
    has_next = seg < segments - 1
    mirrored = wires & (wires - 1) == 0

    def partner(d):
        if not mirrored:
            return lax.rem(me + (d + 1), wires)
        offset, other, bit = wires - 1 - d, me, 1
        while bit <= offset:
            if offset & bit:
                other = other + bit - 2 * bit * lax.rem(lax.div(me, bit), 2)
            bit *= 2
        return other

    def landing(d):
        return d if mirrored else others - 1 - d

    barrier = pltpu.get_barrier_semaphore()
    for d in range(others):
        pl.semaphore_signal(barrier, inc=1, device_id={"wire": partner(d)}, device_id_type=MESH)

    @pl.when(has_prev)
    def _():
        pl.semaphore_signal(barrier, inc=1, device_id={"len": seg - 1}, device_id_type=MESH)

    @pl.when(has_next)
    def _():
        pl.semaphore_signal(barrier, inc=1, device_id={"len": seg + 1}, device_id_type=MESH)

    def match(slots):
        ids = lax.broadcasted_iota(jnp.int32, (wide, LANES), 0).astype(bf16)
        here = jnp.broadcast_to(slots.astype(f32), (2 * SUB, LANES)).astype(bf16)
        here = jnp.concatenate([here] * (wide // (2 * SUB)), axis=0)
        return jnp.where(ids == here, jnp.ones((), bf16), jnp.zeros((), bf16))

    def block_of(slots):
        return (slots * BLOCK_SCALE) >> BLOCK_SHIFT

    def fill(hot, base_ref, at, slots, live):
        count = slots.shape[1]
        which = block_of(slots)
        inside = slots - which * block_slots
        if live is not None:
            which = jnp.where(live > 0, which, -1)
        base_ref[:, at : at + count] = jnp.broadcast_to(which, (SUB, count))
        for start in range(0, count, LANES):
            here = inside[:, start : start + LANES]
            group, lane = divmod(at + start, hot.shape[2])
            hot[group, :, lane : lane + LANES] = match(here)

    for i in FIRST:
        copies[i].wait()
    u_ref[...] = jnp.zeros_like(u_ref)
    p_ref[...] = jnp.zeros_like(p_ref)
    for b in range(blocks):
        lanes = slice(b * block_slots, (b + 1) * block_slots)
        for c in range(parts):
            row = slice(b * SUB + c, b * SUB + c + 1)
            u_ref[row, :block_slots] = u_in[0, c, :, lanes]
    for d in range(others):
        fill(c_hot, cb_ref, d * pairs, slots_in[0, 0, pl.ds(partner(d), 1), :], live_in[0, 0, pl.ds(partner(d), 1), :])

    @pl.when(jnp.logical_not(has_prev))
    def _():
        g_recv[:, 0] = jnp.zeros((ITERS,) + g_recv.shape[2:], f32)

    @pl.when(jnp.logical_not(has_next))
    def _():
        g_recv[:, 1] = jnp.zeros((ITERS,) + g_recv.shape[2:], f32)

    def prepare():
        for i in LATER:
            copies[i].wait()
        row8 = lax.broadcasted_iota(jnp.int32, (SUB, wide), 0)
        lane8 = lax.broadcasted_iota(jnp.int32, (SUB, wide), 1)
        for b in range(blocks):
            at = slice(b * SUB, (b + 1) * SUB)
            lanes = slice(b * block_slots, (b + 1) * block_slots)
            mass_ref[at, :] = jnp.where((row8 == 3) & (lane8 >= block_slots), 1.0, 0.0)
            for c in range(parts):
                p_ref[b * SUB + c : b * SUB + c + 1, :block_slots] = p_in[0, c, :, lanes]
            mass_ref[b * SUB + 3 : b * SUB + 4, :block_slots] = mass_in[0, :, lanes]
        fill(g_hot, gb_ref, 0, left_in[0], None)
        fill(g_hot, gb_ref, ghosts, right_in[0], None)
        op = grad_in[...]
        product = lax.dot_general(
            op, op, (((0,), (0,)), ((), ())), precision=lax.Precision.HIGHEST, preferred_element_type=f32
        )
        high = product.astype(bf16)
        gram[...] = jnp.zeros_like(gram)
        gram[:node_count, :node_count] = high
        gram[:node_count, node_pad : node_pad + node_count] = (product - high.astype(f32)).astype(bf16)
        nodes_ref[...] = jnp.full(nodes_ref.shape, -1, jnp.int32)
        nodes_ref[:, :node_count] = nodes_in[0, 0]
        stiff_ref[...] = jnp.zeros_like(stiff_ref)
        stiff_ref[:, :elements] = jnp.broadcast_to(stiff_in[0], (stiff_ref.shape[0], elements))
        stiff_ref[...] = jnp.transpose(stiff_ref[...])
        for b in range(blocks):
            for e in range(block_elements):
                one = b * block_elements + e
                e_hot[b, :, e * node_pad : (e + 1) * node_pad] = match(nodes_ref[one : one + 1, :])

    last = segments - 1
    pl.semaphore_wait(
        barrier, others + lax.div(seg + last, segments) + lax.div(last - seg + last, segments)
    )

    row_all = lax.broadcasted_iota(jnp.int32, (rows, wide), 0) & (SUB - 1)
    low_all = row_all < 4

    def rows_of(width):
        return lax.broadcasted_iota(jnp.int32, (SUB, width), 0)

    def split(x):
        high = x.astype(bf16).astype(f32)
        return jnp.where(low_all, high, pltpu.roll(x - high, 4, 0)).astype(bf16)

    def take(packed, hot, base_ref, start, width):
        cols = slice(start, start + width)
        picked = dot(packed, hot[start // width])
        which = base_ref[:, cols]
        total = jnp.zeros((SUB, width), f32)
        for b in range(blocks):
            total = jnp.where(which == b, picked[b * SUB : (b + 1) * SUB], total)
        return total + pltpu.roll(total, 4, 0)

    def put(values, hot, base_ref, start, width):
        cols = slice(start, start + width)
        high = values.astype(bf16).astype(f32)
        values = jnp.where(rows_of(width) < 4, high, values - high)
        which = base_ref[:, cols]
        spread = jnp.concatenate([jnp.where(which == b, values, 0.0) for b in range(blocks)], axis=0)
        return dot_nt(spread.astype(bf16), hot[start // width])

    def take_list(packed, hot, base_ref, start, count, out_ref):
        half = count // 2
        width = hot.shape[2]
        for at in range(0, half, width):
            first = take(packed, hot, base_ref, start + at, width)
            second = take(packed, hot, base_ref, start + half + at, width)
            out_ref[:, at : at + width] = jnp.where(rows_of(width) < 4, first, second)

    def put_list(values, hot, base_ref, start, count, total):
        half = count // 2
        width = hot.shape[2]
        for at in range(0, half, width):
            here = values[:, at : at + width]
            turned = pltpu.roll(here, 4, 0)
            low = rows_of(width) < 4
            total = total + put(jnp.where(low, here, turned), hot, base_ref, start + at, width)
            total = total + put(jnp.where(low, turned, here), hot, base_ref, start + half + at, width)
        return total

    def contact_copy(step, d):
        return pltpu.make_async_remote_copy(
            src_ref=c_send.at[d],
            dst_ref=c_recv.at[step, landing(d)],
            send_sem=c_ssem.at[d],
            recv_sem=c_rsem.at[step, landing(d)],
            device_id={"wire": partner(d)},
            device_id_type=MESH,
        )

    def contact_arrival(step, d):
        return pltpu.make_async_remote_copy(
            src_ref=c_send.at[d],
            dst_ref=c_recv.at[step, d],
            send_sem=c_ssem.at[d],
            recv_sem=c_rsem.at[step, d],
            device_id={"wire": partner(d)},
            device_id_type=MESH,
        )

    def ghost_copy(step, side):
        return pltpu.make_async_remote_copy(
            src_ref=g_send.at[side],
            dst_ref=g_recv.at[step, 1 - side],
            send_sem=g_ssem.at[side],
            recv_sem=g_rsem.at[step, 1 - side],
            device_id={"len": seg - 1 if side == 0 else seg + 1},
            device_id_type=MESH,
        )

    def ghost_arrival(step, side):
        return pltpu.make_async_remote_copy(
            src_ref=g_send.at[side],
            dst_ref=g_recv.at[step, side],
            send_sem=g_ssem.at[side],
            recv_sem=g_rsem.at[step, side],
            device_id={"len": seg - 1 if side == 0 else seg + 1},
            device_id_type=MESH,
        )

    exists = (has_prev, has_next)

    def one_step(step, _):
        packed = split(u_ref[...])
        for d in range(others):
            take_list(packed, c_hot, cb_ref, d * pairs, pairs, c_send.at[d])
            contact_copy(step, d).start()

        @pl.when(step == 0)
        def _():
            prepare()

        both = 2 * SUB
        for b in range(blocks):
            pair = packed[(b // 2) * both : (b // 2 + 1) * both]
            out = dot(pair, e_hot[b])[(b % 2) * SUB : (b % 2 + 1) * SUB]
            for e in range(block_elements):
                one = b * block_elements + e
                picked[one * SUB : (one + 1) * SUB, :] = out[:, e * node_pad : (e + 1) * node_pad]
        reach = elements * SUB // 4
        for at in range(0, elements * SUB, reach):
            out = dot(picked[at : at + reach, :].astype(bf16), gram[...])
            main = out[:, :node_pad]
            main = main + pltpu.roll(main, reach - 4, 0) + out[:, node_pad:]
            for i in range(0, reach, SUB):
                one = (at + i) // SUB
                r = main[i : i + SUB] * jnp.broadcast_to(stiff_ref[one : one + 1, :], (SUB, node_pad))
                high = r.astype(bf16).astype(f32)
                low = jnp.where(rows_of(node_pad) < 4, high, pltpu.roll(r - high, 4, 0))
                picked[at + i : at + i + SUB, :] = low
        for b in range(0, blocks, 2):
            pair = jnp.concatenate(
                [
                    jnp.concatenate(
                        [
                            picked[one * SUB : (one + 1) * SUB, :]
                            for one in range(k * block_elements, (k + 1) * block_elements)
                        ],
                        axis=1,
                    )
                    for k in (b, b + 1)
                ],
                axis=0,
            ).astype(bf16)
            for k in range(2):
                out = dot_nt(pair, e_hot[b + k])[k * SUB : (k + 1) * SUB]
                part[(b + k) * SUB : (b + k + 1) * SUB, :] = out + pltpu.roll(out, 4, 0)

        spread = jnp.zeros((rows, wide), f32)
        for d in reversed(range(others)):
            contact_arrival(step, d).wait_recv()
            spread = put_list(c_recv[step, d] - c_send[d], c_hot, cb_ref, d * pairs, pairs, spread)
        spread = spread + pltpu.roll(spread, rows - 4, 0)
        local = jnp.where(row_all < 3, PENALTY * spread - part[...], mass_ref[...])
        part[...] = local

        packed = split(local)
        for side in range(2):
            take_list(packed, g_hot, gb_ref, side * ghosts, ghosts, g_send.at[side])

            @pl.when(exists[side])
            def _():
                ghost_copy(step, side).start()

        spread = jnp.zeros((rows, wide), f32)
        for side in range(2):

            @pl.when(exists[side])
            def _():
                ghost_arrival(step, side).wait_recv()

            spread = put_list(g_recv[step, side], g_hot, gb_ref, side * ghosts, ghosts, spread)
        spread = spread + pltpu.roll(spread, rows - 4, 0)
        total = jnp.where(low_all, part[...] + spread, 0.0)
        for b in range(blocks):
            at = slice(b * SUB, (b + 1) * SUB)
            force = total[at]
            mass = jnp.broadcast_to(force[3:4], force.shape)
            now = u_ref[at, :]
            stepped = 2.0 * now - p_ref[at, :] + TIME_SQUARE * force / mass
            p_ref[at, :] = now
            u_ref[at, :] = jnp.where(rows_of(wide) < 3, stepped, 0.0)

        for d in range(others):
            contact_copy(step, d).wait_send()
        for side in range(2):

            @pl.when(exists[side])
            def _():
                ghost_copy(step, side).wait_send()

        return 0

    lax.fori_loop(0, ITERS, one_step, 0)
    for b in range(blocks):
        lanes = slice(b * block_slots, (b + 1) * block_slots)
        for c in range(parts):
            row = slice(b * SUB + c, b * SUB + c + 1)
            u_out[0, c, :, lanes] = u_ref[row, :block_slots]
            p_out[0, c, :, lanes] = p_ref[row, :block_slots]


def on_device(displacement, previous, element_nodes, *rest):
    left_ghost, contact_slots = rest[3], rest[5]
    node_count, elements = element_nodes.shape[2:]
    blocks = elements // block_elements
    wide = round_up(block_slots, 2 * LANES)
    node_pad = round_up(node_count, LANES)
    wires = lax.axis_size("wire")
    others = wires - 1
    rows = blocks * SUB
    pairs = contact_slots.shape[3]
    ghosts = left_ghost.shape[2]
    c_width, g_width = (512 if x % 512 == 0 else x for x in (pairs // 2, ghosts // 2))
    assert blocks % 2 == 0 and elements <= LANES and node_pad == LANES
    assert all((x * BLOCK_SCALE) >> BLOCK_SHIFT == x // block_slots for x in range(blocks * block_slots))

    vmem = pl.BlockSpec(memory_space=pltpu.VMEM)
    turned = jnp.swapaxes(displacement, 1, 2)
    args = (turned, jnp.swapaxes(previous, 1, 2), jnp.swapaxes(element_nodes, 2, 3), *rest)
    results = pl.pallas_call(
        functools.partial(step_kernel, wires, lax.axis_size("len"), 512),
        out_shape=[jax.ShapeDtypeStruct(turned.shape, f32)] * 2,
        in_specs=[pl.BlockSpec(memory_space=pl.ANY)] * len(args),
        out_specs=[vmem] * 2,
        scratch_shapes=[pltpu.VMEM(x.shape, x.dtype) for x in args]
        + [pltpu.SemaphoreType.DMA((len(args),))]
        + [
            pltpu.VMEM((rows, wide), f32),
            pltpu.VMEM((rows, wide), f32),
            pltpu.VMEM((rows, wide), f32),
            pltpu.VMEM((others * pairs // c_width, wide, c_width), bf16),
            pltpu.VMEM((2 * ghosts // g_width, wide, g_width), bf16),
            pltpu.VMEM((blocks, wide, block_elements * node_pad), bf16),
            pltpu.VMEM((SUB, others * pairs), jnp.int32),
            pltpu.VMEM((SUB, 2 * ghosts), jnp.int32),
            pltpu.VMEM((node_pad, 2 * node_pad), bf16),
            pltpu.VMEM((elements, node_pad), jnp.int32),
            pltpu.VMEM((LANES, LANES), f32),
            pltpu.VMEM((rows, wide), f32),
            pltpu.VMEM((elements * SUB, node_pad), f32),
            pltpu.VMEM((others, SUB, pairs // 2), f32),
            pltpu.VMEM((ITERS, others, SUB, pairs // 2), f32),
            pltpu.VMEM((2, SUB, ghosts // 2), f32),
            pltpu.VMEM((ITERS, 2, SUB, ghosts // 2), f32),
            pltpu.SemaphoreType.DMA((others,)),
            pltpu.SemaphoreType.DMA((ITERS, others)),
            pltpu.SemaphoreType.DMA((2,)),
            pltpu.SemaphoreType.DMA((ITERS, 2)),
        ],
        compiler_params=pltpu.CompilerParams(
            collective_id=0, has_side_effects=True, vmem_limit_bytes=VMEM_BYTES
        ),
        name="steps",
    )(*args)
    return tuple(jnp.swapaxes(x, 1, 2) for x in results)


def solution(mesh):
    four = P("len", "wire", None, None)
    three = P("len", "wire", None)
    return jax.shard_map(
        on_device,
        mesh=mesh,
        in_specs=(four, four, four, three, P(), three, three, three, four, four),
        out_specs=(four, four),
        check_vma=False,
    )
```
